32 devices in a mesh: groups: 2 (over y), cuts: 16 (over z, x, core).
Axes of the slice: x: 2, y: 2, z: 4, core: 2. Of those that a mesh axis runs over, the one named last changes fastest.
Arguments:
- estimate: float32 [4, 16, 128, 256], P('groups', 'cuts'), parts along dimension 0, may hold values from -6 to 6
- coil_maps: float32 [4, 16, 16, 128, 256], P('groups', None, 'cuts'), parts along dimension 0, may hold values from -3 to 3
- measured: float32 [4, 16, 16, 128, 256], P('groups', None, None, 'cuts'), parts along dimension 0, may hold values from -5 to 5
- sampled: int32 [32, 128], P('groups', 'cuts'), parts along dimension 0, may hold values 0 or 1
- plane_kernel: bfloat16 [3, 3, 2, 48], replicated, may hold values from -1.5 to 1.5
- depth_kernel: bfloat16 [3, 48, 48], replicated, may hold values from -0.5 to 0.5
- depth_offset: float32 [48], replicated, may hold values from -3 to 3
Outputs:
- next_image: float32 [4, 16, 128, 256], P('groups', 'cuts'), parts along dimension 0
The draws below stay inside these ranges and needn't reach their ends.
There are 2 independent parts, one for each index of `groups`. The reference program is written for one: setup_inputs(seed, part) draws one part's arguments, and reference() takes and returns one part's arrays. A program takes and returns all parts, laid end to end along the dimension named above; an argument that names none is the same for every part. Nothing has to cross between parts.
All inputs are finite; a program needn't handle non-finite values. No bound on the sum of `sampled` on one device may be relied on, other than what follows from the above.
Results may differ from the reference program's by a relative error of at most 0.0027.
Values may be sent and summed in bfloat16 or wider, within the bound.
No kernel may reach another device: no remote copies, remote signals or barrier semaphores. Data moves between devices by JAX's collectives and lax.ppermute only.
A program may use at most 128 MiB of HBM per device.

```python
import jax
import jax.numpy as jnp
from jax import lax

NX = 256
NY = 128
COILS = 16
CH = 48
NZ = 16


def set_ends(array, rng, least, top_value):
    place = [jax.random.randint(jax.random.fold_in(rng, axis), (), 0, length) for axis, length in enumerate(array.shape)]
    longest = array.shape.index(max(array.shape))
    next_to = place[:longest] + [(place[longest] + 1) % array.shape[longest]] + place[longest + 1:]
    return array.at[tuple(place)].set(least).at[tuple(next_to)].set(top_value)


def level_of(key, extent, pieces, low, high):
    level = 1.0
    for position, shards_of in pieces:
        draws = jax.random.uniform(jax.random.fold_in(jax.random.fold_in(key, 6), position), (shards_of,), jnp.float32, low / len(pieces), high / len(pieces))
        level = level * jnp.repeat(jnp.exp(draws), extent[position] // shards_of).reshape((-1,) + (1,) * (len(extent) - 1 - position))
    return level


def normal_values(rng, shape, scale, reach, shards=(), kind=jnp.bfloat16):
    drawn = jax.random.normal(rng, shape, jnp.float32) * scale
    if len(shards) > 0:
        drawn = level_of(rng, shape, shards, -0.22, 0.18) * drawn
    return jnp.clip(drawn, min=-reach, max=reach).astype(kind)


def setup_inputs(seed: int = 0, part: int = 0) -> dict:
    splits = jax.random.split(jax.random.key(seed), 8)
    part_keys = jax.random.split(jax.random.fold_in(splits[7], part), 8)
    estimate = normal_values(part_keys[0], (2, NZ, NY, NX), 1.0, 6.0, ((1, 16),), jnp.float32)
    coil_maps = normal_values(part_keys[1], (2, COILS, NZ, NY, NX), 0.5, 3.0, ((2, 16),), jnp.float32)
    measured = normal_values(part_keys[2], (2, COILS, NZ, NY, NX), 0.7, 5.0, ((3, 16),), jnp.float32)
    sampled = set_ends((jax.random.randint(part_keys[3], (NZ, NY), 0, 3) < 1).astype(jnp.int32), jax.random.fold_in(part_keys[3], 1), 0, 1)
    plane_kernel = normal_values(splits[4], (3, 3, 2, CH), 18 ** -0.5, 1.5)
    depth_kernel = normal_values(splits[5], (3, CH, CH), (3 * CH) ** -0.5, 0.5)
    depth_offset = normal_values(splits[6], (CH,), 0.5, 3.0, (), jnp.float32)
    return {"estimate": estimate, "coil_maps": coil_maps, "measured": measured, "sampled": sampled, "plane_kernel": plane_kernel, "depth_kernel": depth_kernel, "depth_offset": depth_offset}


def plane_conv(volume, kernel):
    rows, columns = volume.shape[2], volume.shape[3]
    padded = jnp.pad(volume, ((0, 0), (0, 0), (1, 1), (1, 1)))
    summed = None
    for row_shift in range(3):
        for column_shift in range(3):
            piece = padded[:, :, row_shift:row_shift + rows, column_shift:column_shift + columns]
            term = jnp.einsum("ic,izyx->czyx", kernel[row_shift, column_shift], piece, precision=lax.Precision.HIGHEST)
            summed = term if summed is None else summed + term
    return summed


def plane_adjoint(volume, kernel):
    rows, columns = volume.shape[2], volume.shape[3]
    padded = jnp.pad(volume, ((0, 0), (0, 0), (1, 1), (1, 1)))
    summed = None
    for row_shift in range(3):
        for column_shift in range(3):
            piece = padded[:, :, 2 - row_shift:2 - row_shift + rows, 2 - column_shift:2 - column_shift + columns]
            term = jnp.einsum("ic,czyx->izyx", kernel[row_shift, column_shift], piece, precision=lax.Precision.HIGHEST)
            summed = term if summed is None else summed + term
    return summed


def reference(estimate, coil_maps, measured, sampled, plane_kernel, depth_kernel, depth_offset):
    ftype = estimate.dtype
    image_bf = estimate.astype(jnp.bfloat16)
    plane_wide = plane_kernel.astype(ftype)
    depth_wide = depth_kernel.astype(ftype)
    features = plane_conv(image_bf.astype(ftype), plane_wide).astype(jnp.bfloat16)
    padded_feat = jnp.pad(features.astype(ftype), ((0, 0), (1, 1), (0, 0), (0, 0)))
    preact = depth_offset[:, None, None, None]
    for tap_index in range(3):
        preact = preact + jnp.einsum("ic,izyx->czyx", depth_wide[tap_index], padded_feat[:, tap_index:tap_index + NZ], precision=lax.Precision.HIGHEST)
    activation = jnp.tanh(preact).astype(jnp.bfloat16)
    padded_act = jnp.pad(activation.astype(ftype), ((0, 0), (1, 1), (0, 0), (0, 0)))
    backward_mix = None
    for tap_index in range(3):
        term = jnp.einsum("ic,czyx->izyx", depth_wide[tap_index], padded_act[:, 2 - tap_index:2 - tap_index + NZ], precision=lax.Precision.HIGHEST)
        backward_mix = term if backward_mix is None else backward_mix + term
    regular = plane_adjoint(backward_mix, plane_wide)
    picture = estimate[0] + 1j * estimate[1]
    maps = coil_maps[0] + 1j * coil_maps[1]
    coil_images = maps * picture[None]
    kspace = jnp.fft.fftn(coil_images, axes=(1, 2, 3), norm="ortho")
    keep_mask = sampled.astype(ftype)[None, :, :, None]
    residual = keep_mask * (kspace - (measured[0] + 1j * measured[1]))
    errors = jnp.fft.ifftn(residual, axes=(1, 2, 3), norm="ortho")
    gradient = jnp.sum(jnp.conj(maps) * errors, axis=0)
    grad_parts = jnp.stack([jnp.real(gradient), jnp.imag(gradient)]).astype(ftype)
    return (estimate - 0.5 * grad_parts - 0.25 * regular).astype(jnp.float32)
```

```python
import math

import jax
import jax.numpy as jnp
import numpy as np
from jax import lax
from jax.experimental import pallas as pl
from jax.experimental.pallas import tpu as pltpu
from jax.sharding import PartitionSpec as P

step_size = 0.5
reg_weight = 0.25

f32 = jnp.float32
bf16 = jnp.bfloat16


def with_halo(x, sides, width):
    for axis, dim in sides:
        devices, length = (lax.axis_size(axis), x.shape[dim])
        up = [(i, (i + 1) % devices) for i in range(devices - 1)]
        down = [(j, i) for i, j in up]
        last = lax.slice_in_dim(x, length - width, length, axis=dim)
        initial = lax.slice_in_dim(x, 0, width, axis=dim)
        before = lax.ppermute(last, axis, up)
        after = lax.ppermute(initial, axis, down)
        x = jnp.concatenate([before, x, after], axis=dim)
    return x


def shifted_2(value, axis, steps):
    count = lax.axis_size(axis)
    initial, last = (max(0, -steps), min(count, count - steps))
    return lax.ppermute(value, axis, [(source, source + steps) for source in range(initial, last)])


def plane_conv(volume, kernel):
    rows, columns = (volume.shape[2], volume.shape[3])
    padded = jnp.pad(volume, ((0, 0), (0, 0), (1, 1), (1, 1)))
    shifted = jnp.concatenate(
        [
            padded[:, :, row_shift : row_shift + rows, column_shift : column_shift + columns]
            for row_shift in range(3)
            for column_shift in range(3)
        ],
        axis=0,
    )
    flat_kernel = kernel.reshape(9 * kernel.shape[2], kernel.shape[3])
    return jnp.einsum("kc,kzyx->czyx", flat_kernel, shifted, preferred_element_type=jnp.float32)


def plane_adjoint(volume, kernel):
    rows, columns = (volume.shape[2], volume.shape[3])
    padded = jnp.pad(volume, ((0, 0), (0, 0), (1, 1), (1, 1)))
    summed = None
    for row_shift in range(3):
        for column_shift in range(3):
            piece = padded[
                :,
                :,
                2 - row_shift : 2 - row_shift + rows,
                2 - column_shift : 2 - column_shift + columns,
            ]
            term = jnp.einsum(
                "ic,czyx->izyx",
                kernel[row_shift, column_shift],
                piece,
                precision=lax.Precision.HIGHEST,
            )
            summed = term if summed is None else summed + term
    return summed


def transform(real_part, imag_part, pattern, length, inverse):
    index = jnp.arange(length, dtype=jnp.int32)
    angles = (index[:, None] * index[None, :] % length).astype(jnp.float32) * (
        2.0 * math.pi / length
    )
    factor = 1.0 / math.sqrt(length)
    cosine_table = jnp.cos(angles) * factor
    sine_table = jnp.sin(angles) * factor

    def multiply(volume, table):
        return jnp.einsum(pattern, volume, table, precision=lax.Precision.HIGHEST)

    if inverse:
        return (
            multiply(real_part, cosine_table) - multiply(imag_part, sine_table),
            multiply(imag_part, cosine_table) + multiply(real_part, sine_table),
        )
    return (
        multiply(real_part, cosine_table) + multiply(imag_part, sine_table),
        multiply(imag_part, cosine_table) - multiply(real_part, sine_table),
    )


def depth_forward(pieces):
    real_part, imag_part = transform(pieces[0], pieces[1], "czyx,zk->ckyx", pieces.shape[2], False)
    return jnp.stack([real_part, imag_part])


def plane_inverse(pieces):
    real_part, imag_part = transform(pieces[0], pieces[1], "czyx,yk->czkx", pieces.shape[3], True)
    real_part, imag_part = transform(real_part, imag_part, "czyx,xk->czyk", pieces.shape[4], True)
    return jnp.stack([real_part, imag_part])


def general_shards(
    estimate, coil_maps, measured, sampled, plane_kernel, depth_kernel, depth_offset
):
    slices = estimate.shape[1]
    image_bf = estimate.astype(jnp.bfloat16)
    features = plane_conv(image_bf, plane_kernel).astype(jnp.bfloat16)
    padded_feat = with_halo(features, (("cuts", 1),), 1)
    preact = depth_offset[:, None, None, None]
    for tap_index in range(3):
        preact = preact + jnp.einsum(
            "ic,izyx->czyx",
            depth_kernel[tap_index],
            padded_feat[:, tap_index : tap_index + slices],
            preferred_element_type=jnp.float32,
        )
    activation = jnp.tanh(preact).astype(jnp.bfloat16)
    plane_wide = plane_kernel.astype(jnp.float32)
    projected = [
        plane_adjoint(
            jnp.einsum(
                "ic,czyx->izyx",
                depth_kernel[tap_index],
                activation,
                preferred_element_type=jnp.float32,
            ),
            plane_wide,
        )
        for tap_index in range(3)
    ]
    from_below = shifted_2(projected[2], "cuts", 1)
    from_above = shifted_2(projected[0], "cuts", -1)
    regular = projected[1] + jnp.concatenate([from_below, projected[2][:, : slices - 1]], axis=1)
    regular = regular + jnp.concatenate([projected[0][:, 1:], from_above], axis=1)
    maps_real, maps_imag = (coil_maps[0], coil_maps[1])
    image_real, image_imag = (estimate[0][None], estimate[1][None])
    coil_real = maps_real * image_real - maps_imag * image_imag
    coil_imag = maps_real * image_imag + maps_imag * image_real
    coil_real, coil_imag = transform(
        coil_real, coil_imag, "czyx,xk->czyk", coil_real.shape[3], False
    )
    coil_real, coil_imag = transform(
        coil_real, coil_imag, "czyx,yk->czkx", coil_real.shape[2], False
    )
    stacked = jnp.stack([coil_real, coil_imag])
    kspace = depth_forward(lax.all_to_all(stacked, "cuts", split_axis=3, concat_axis=2, tiled=True))
    keep_mask = sampled.astype(jnp.float32)[None, None, :, :, None]
    residual = keep_mask * (kspace - measured)
    depth_real, depth_imag = transform(
        residual[0], residual[1], "czyx,zk->ckyx", residual.shape[2], True
    )
    errors = plane_inverse(
        lax.all_to_all(
            jnp.stack([depth_real, depth_imag]), "cuts", split_axis=2, concat_axis=3, tiled=True
        )
    )
    grad_real = jnp.sum(maps_real * errors[0] + maps_imag * errors[1], axis=0)
    grad_imag = jnp.sum(maps_real * errors[1] - maps_imag * errors[0], axis=0)
    gradient = jnp.stack([grad_real, grad_imag])
    return estimate - step_size * gradient - reg_weight * regular


def dft_tables(length):
    index = np.arange(length)
    angles = 2.0 * np.pi * ((index[:, None] * index[None, :]) % length) / length
    factor = 1.0 / np.sqrt(length)
    return np.cos(angles) * factor, np.sin(angles) * factor


def two_parts(table):
    table = table.astype(np.float32)
    high = table.astype(bf16)
    return high, (table - high.astype(np.float32)).astype(bf16)


def line_order(length, devices):
    lines = length // devices
    order = np.arange(2 * length).reshape(2, devices, lines)
    return order.transpose(1, 0, 2).reshape(-1)


def line_table(length, devices, slab):
    cosine, sine = dft_tables(length)
    full = np.block([[cosine, sine], [-sine, cosine]]) / np.sqrt(slab)
    return two_parts(full[line_order(length, devices)])


def line_table_back(length, devices, slab):
    cosine, sine = dft_tables(length)
    full = np.block([[cosine, -sine], [sine, cosine]]) / np.sqrt(slab)
    return two_parts(full[:, line_order(length, devices)])


def readout_table(length):
    cosine, sine = dft_tables(length)
    return two_parts(np.block([[cosine, sine], [-sine, cosine]]))


def fft_list(real, imag, sign):
    count = len(real)
    if count == 1:
        return real, imag
    even_r, even_i = fft_list(real[0::2], imag[0::2], sign)
    odd_r, odd_i = fft_list(real[1::2], imag[1::2], sign)
    half = count // 2
    low_r, low_i, high_r, high_i = [], [], [], []
    for k in range(half):
        a, b = odd_r[k], odd_i[k]
        if k == 0:
            tr, ti = a, b
        elif 4 * k == count:
            tr, ti = (b, -a) if sign < 0 else (-b, a)
        elif 8 * k == count or 8 * k == 3 * count:
            h = math.sqrt(0.5)
            c = h if 8 * k == count else -h
            s = sign * h
            if c > 0:
                tr, ti = ((a - b) * h, (a + b) * h) if s > 0 else ((a + b) * h, (b - a) * h)
            else:
                tr, ti = ((a + b) * (-h), (a - b) * h) if s > 0 else ((b - a) * h, (a + b) * (-h))
        else:
            c = math.cos(2.0 * math.pi * k / count)
            s = sign * math.sin(2.0 * math.pi * k / count)
            tr, ti = a * c - b * s, a * s + b * c
        low_r.append(even_r[k] + tr)
        low_i.append(even_i[k] + ti)
        high_r.append(even_r[k] - tr)
        high_i.append(even_i[k] - ti)
    return low_r + high_r, low_i + high_i


def dot(a, b):
    return jnp.dot(a, b, preferred_element_type=f32)


def whole_block(shape):
    return pl.BlockSpec(shape, lambda *_: (0,) * len(shape))


def coil_lines(coil_maps, estimate, devices, slab, per_step):
    _, coils, _, rows, columns = coil_maps.shape
    high, low = line_table(rows, devices, slab)

    def kernel(maps_ref, image_ref, high_ref, low_ref, out_ref):
        image_r, image_i = image_ref[0, 0], image_ref[1, 0]
        for c in range(per_step):
            map_r, map_i = maps_ref[0, c, 0], maps_ref[1, c, 0]
            coil = jnp.concatenate(
                [map_r * image_r - map_i * image_i, map_r * image_i + map_i * image_r], axis=0
            ).astype(bf16)
            lines = dot(high_ref[...], coil) + dot(low_ref[...], coil)
            out_ref[:, c] = lines.astype(bf16).reshape(devices, 2 * rows // devices, columns)

    return pl.pallas_call(
        kernel,
        out_shape=jax.ShapeDtypeStruct((devices, coils, 2 * rows // devices, columns), bf16),
        grid=(coils // per_step,),
        in_specs=[
            pl.BlockSpec((2, per_step, 1, rows, columns), lambda i: (0, i, 0, 0, 0)),
            whole_block(estimate.shape),
            whole_block(high.shape),
            whole_block(low.shape),
        ],
        out_specs=pl.BlockSpec(
            (devices, per_step, 2 * rows // devices, columns), lambda i: (0, i, 0, 0)
        ),
        name="coil_lines",
    )(coil_maps, estimate, high, low)


def measured_readout(measured, per_step):
    _, coils, slab, lines, columns = measured.shape
    high, low = readout_table(columns)

    def kernel(data_ref, high_ref, low_ref, out_ref):
        rows = per_step * slab * lines
        data = jnp.concatenate(
            [data_ref[0].reshape(rows, columns), data_ref[1].reshape(rows, columns)], axis=1
        ).astype(bf16)
        result = dot(data, high_ref[...]) + dot(data, low_ref[...])
        for part in range(2):
            piece = result[:, part * columns : (part + 1) * columns]
            out_ref[:, :, part] = piece.reshape(per_step, slab, lines, columns)

    return pl.pallas_call(
        kernel,
        out_shape=jax.ShapeDtypeStruct((coils, slab, 2, lines, columns), f32),
        grid=(coils // per_step,),
        in_specs=[
            pl.BlockSpec((2, per_step, slab, lines, columns), lambda i: (0, i, 0, 0, 0)),
            whole_block(high.shape),
            whole_block(low.shape),
        ],
        out_specs=pl.BlockSpec((per_step, slab, 2, lines, columns), lambda i: (i, 0, 0, 0, 0)),
        name="measured_readout",
    )(measured, high, low)


def depth_residual(lines_in, readout, keep, per_step):
    slab, coils, double, columns = lines_in.shape
    lines = double // 2
    width = 128

    def kernel(in_ref, data_ref, keep_ref, out_ref):
        def one(step, carry):
            c = step // (columns // width)
            at = pl.ds(pl.multiple_of((step % (columns // width)) * width, width), width)
            loaded = [in_ref[z, c, :, at].astype(f32) for z in range(slab)]
            real, imag = fft_list([v[:lines] for v in loaded], [v[lines:] for v in loaded], -1)
            for k in range(slab):
                mask = keep_ref[k]
                real[k] = mask * (real[k] - data_ref[c, k, 0, :, at])
                imag[k] = mask * (imag[k] - data_ref[c, k, 1, :, at])
            real, imag = fft_list(real, imag, 1)
            for z in range(slab):
                out_ref[z, c, :, at] = jnp.concatenate([real[z], imag[z]], axis=0).astype(bf16)
            return carry

        lax.fori_loop(0, per_step * (columns // width), one, 0)

    return pl.pallas_call(
        kernel,
        out_shape=jax.ShapeDtypeStruct(lines_in.shape, bf16),
        grid=(coils // per_step,),
        in_specs=[
            pl.BlockSpec((slab, per_step, double, columns), lambda i: (0, i, 0, 0)),
            pl.BlockSpec((per_step, slab, 2, lines, columns), lambda i: (i, 0, 0, 0, 0)),
            whole_block(keep.shape),
        ],
        out_specs=pl.BlockSpec((slab, per_step, double, columns), lambda i: (0, i, 0, 0)),
        name="depth_residual",
    )(lines_in, readout, keep)


def image_update(lines_back, coil_maps, estimate, regular, slab, per_step):
    devices, coils, double, columns = lines_back.shape
    rows = coil_maps.shape[3]
    high, low = line_table_back(rows, devices, slab)

    def kernel(lines_ref, maps_ref, image_ref, regular_ref, high_ref, low_ref, out_ref):
        step = pl.program_id(0)

        @pl.when(step == 0)
        def _():
            out_ref[...] = image_ref[...] - reg_weight * regular_ref[...]

        sum_r = sum_i = None
        for c in range(per_step):
            lines = lines_ref[:, c].reshape(devices * double, columns)
            errors = dot(high_ref[...], lines) + dot(low_ref[...], lines)
            error_r, error_i = errors[:rows], errors[rows:]
            map_r, map_i = maps_ref[0, c, 0], maps_ref[1, c, 0]
            term_r = map_r * error_r + map_i * error_i
            term_i = map_r * error_i - map_i * error_r
            sum_r = term_r if sum_r is None else sum_r + term_r
            sum_i = term_i if sum_i is None else sum_i + term_i
        out_ref[0, 0] = out_ref[0, 0] - step_size * sum_r
        out_ref[1, 0] = out_ref[1, 0] - step_size * sum_i

    return pl.pallas_call(
        kernel,
        out_shape=jax.ShapeDtypeStruct(estimate.shape, f32),
        grid=(coils // per_step,),
        in_specs=[
            pl.BlockSpec((devices, per_step, double, columns), lambda i: (0, i, 0, 0)),
            pl.BlockSpec((2, per_step, 1, rows, columns), lambda i: (0, i, 0, 0, 0)),
            whole_block(estimate.shape),
            whole_block(regular.shape),
            whole_block(high.shape),
            whole_block(low.shape),
        ],
        out_specs=whole_block(estimate.shape),
        name="image_update",
    )(lines_back, coil_maps, estimate, regular, high, low)


def regularizer(images, plane_kernel, depth_kernel, depth_offset, columns):
    points = images.shape[1]
    channels = plane_kernel.shape[3]
    block = 2048 if points % 2048 == 0 else columns
    plane_wide = plane_kernel.astype(f32).reshape(9, 2, channels)
    depth_wide = depth_kernel.astype(f32)
    spread = jnp.eye(3, dtype=f32)
    features_of = jnp.einsum("st,ric->scrti", spread, plane_wide).reshape(3 * channels, 9, 6)
    features_of = jnp.pad(features_of, ((0, 0), (0, 0), (0, 2)))
    features_of = features_of.reshape(3 * channels, 72).astype(bf16)
    mix = depth_wide.transpose(2, 0, 1).reshape(channels, 3 * channels).astype(bf16)
    back = jnp.einsum("rij,kjc->rkic", plane_wide, depth_wide, precision=lax.Precision.HIGHEST)
    back = jnp.pad(back.reshape(9, 6, channels), ((0, 0), (0, 2), (0, 0))).reshape(72, channels)
    back_high = back.astype(bf16)
    back_low = (back - back_high.astype(f32)).astype(bf16)
    offset = jnp.broadcast_to(depth_offset[:, None], (channels, 128))

    def kernel(image_ref, features_ref, mix_ref, high_ref, low_ref, offset_ref, out_ref, taps_ref, sums_ref):
        image = image_ref[...].astype(f32)
        column = lax.broadcasted_iota(jnp.int32, (8, points), 1) % columns
        edge = jnp.zeros((8, columns), f32)
        left = jnp.where(column == 0, 0.0, pltpu.roll(image, 1, 1))
        right = jnp.where(column == columns - 1, 0.0, pltpu.roll(image, points - 1, 1))
        for b, moved in enumerate((left, image, right)):
            taps_ref[b, :, :columns] = edge
            taps_ref[b, :, columns : columns + points] = moved
            taps_ref[b, :, columns + points :] = edge
        sums_ref[...] = jnp.zeros(sums_ref.shape, f32)
        bias = offset_ref[:, :1]

        def one(j, carry):
            def at(a):
                return pl.ds(pl.multiple_of(j * block + a * columns, 128), block)

            taps = jnp.concatenate(
                [taps_ref[b, :, at(a)] for a in range(3) for b in range(3)], axis=0
            ).astype(bf16)
            features = dot(features_ref[...], taps).astype(bf16)
            activation = jnp.tanh(dot(mix_ref[...], features) + bias).astype(bf16)
            spread_back = dot(high_ref[...], activation) + dot(low_ref[...], activation)
            for a in range(3):
                for b in range(3):
                    row = 8 * (3 * a + b)
                    sums_ref[b, :, at(a)] = sums_ref[b, :, at(a)] + spread_back[row : row + 8]
            return carry

        lax.fori_loop(0, points // block, one, 0)
        inside = slice(columns, columns + points)
        from_right = pltpu.roll(sums_ref[0, :, inside], points - 1, 1)
        from_left = pltpu.roll(sums_ref[2, :, inside], 1, 1)
        out_ref[...] = (
            sums_ref[1, :, inside]
            + jnp.where(column == columns - 1, 0.0, from_right)
            + jnp.where(column == 0, 0.0, from_left)
        )

    padded = points + 2 * columns
    return pl.pallas_call(
        kernel,
        out_shape=jax.ShapeDtypeStruct((8, points), f32),
        scratch_shapes=[pltpu.VMEM((3, 8, padded), f32), pltpu.VMEM((3, 8, padded), f32)],
        name="regularizer",
    )(images, features_of, mix, back_high, back_low, offset)


def fast_shards(estimate, coil_maps, measured, sampled, plane_kernel, depth_kernel, depth_offset):
    devices = lax.axis_size("cuts")
    _, coils, _, rows, columns = coil_maps.shape
    slab, lines = sampled.shape
    points = rows * columns
    up = [(i, i + 1) for i in range(devices - 1)]
    down = [(i + 1, i) for i in range(devices - 1)]

    coil_side = coil_lines(coil_maps, estimate, devices, slab, 4)
    line_side = lax.all_to_all(coil_side, "cuts", 0, 0, tiled=True)

    image_bf = estimate.astype(bf16)
    below = lax.ppermute(image_bf, "cuts", up)
    above = lax.ppermute(image_bf, "cuts", down)
    images = jnp.concatenate([below, image_bf, above], axis=0).reshape(6, points)
    images = jnp.pad(images, ((0, 2), (0, 0)))
    parts = regularizer(images, plane_kernel, depth_kernel, depth_offset, columns)
    parts = parts[:6].reshape(3, 2, 1, rows, columns)
    regular = parts[1] + lax.ppermute(parts[2], "cuts", up) + lax.ppermute(parts[0], "cuts", down)

    readout = measured_readout(measured, 4)
    keep = jnp.broadcast_to(sampled.astype(f32)[:, :, None], (slab, lines, 128))
    residual = depth_residual(line_side, readout, keep, 4)
    lines_back = lax.all_to_all(residual, "cuts", 0, 0, tiled=True)
    return image_update(lines_back, coil_maps, estimate, regular, slab, 4)


def shards(estimate, coil_maps, measured, sampled, plane_kernel, depth_kernel, depth_offset):
    devices = lax.axis_size("cuts")
    slab, lines = sampled.shape
    coils, slices = coil_maps.shape[1:3]
    fits = (
        slices == 1
        and slab == devices
        and slab & (slab - 1) == 0
        and lines % 8 == 0
        and coils % 4 == 0
        and estimate.shape[3] % 128 == 0
    )
    chosen = fast_shards if fits else general_shards
    return chosen(
        estimate, coil_maps, measured, sampled, plane_kernel, depth_kernel, depth_offset
    )


def solution(mesh):
    return jax.shard_map(
        shards,
        mesh=mesh,
        in_specs=(
            P("groups", "cuts", None, None),
            P("groups", None, "cuts", None, None),
            P("groups", None, None, "cuts", None),
            P("groups", "cuts"),
            P(),
            P(),
            P(),
        ),
        out_specs=P("groups", "cuts", None, None),
        check_vma=False,
    )
```

```python
import math

import jax
import jax.numpy as jnp
import numpy as np
from jax import lax
from jax.experimental import pallas as pl
from jax.experimental.pallas import tpu as pltpu
from jax.sharding import PartitionSpec as P

step_size = 0.5
reg_weight = 0.25

f32 = jnp.float32
bf16 = jnp.bfloat16


def with_halo(x, sides, width):
    for axis, dim in sides:
        devices, length = (lax.axis_size(axis), x.shape[dim])
        up = [(i, (i + 1) % devices) for i in range(devices - 1)]
        down = [(j, i) for i, j in up]
        last = lax.slice_in_dim(x, length - width, length, axis=dim)
        initial = lax.slice_in_dim(x, 0, width, axis=dim)
        before = lax.ppermute(last, axis, up)
        after = lax.ppermute(initial, axis, down)
        x = jnp.concatenate([before, x, after], axis=dim)
    return x


def shifted_2(value, axis, steps):
    count = lax.axis_size(axis)
    initial, last = (max(0, -steps), min(count, count - steps))
    return lax.ppermute(value, axis, [(source, source + steps) for source in range(initial, last)])


def plane_conv(volume, kernel):
    rows, columns = (volume.shape[2], volume.shape[3])
    padded = jnp.pad(volume, ((0, 0), (0, 0), (1, 1), (1, 1)))
    shifted = jnp.concatenate(
        [
            padded[:, :, row_shift : row_shift + rows, column_shift : column_shift + columns]
            for row_shift in range(3)
            for column_shift in range(3)
        ],
        axis=0,
    )
    flat_kernel = kernel.reshape(9 * kernel.shape[2], kernel.shape[3])
    return jnp.einsum("kc,kzyx->czyx", flat_kernel, shifted, preferred_element_type=jnp.float32)


def plane_adjoint(volume, kernel):
    rows, columns = (volume.shape[2], volume.shape[3])
    padded = jnp.pad(volume, ((0, 0), (0, 0), (1, 1), (1, 1)))
    summed = None
    for row_shift in range(3):
        for column_shift in range(3):
            piece = padded[
                :,
                :,
                2 - row_shift : 2 - row_shift + rows,
                2 - column_shift : 2 - column_shift + columns,
            ]
            term = jnp.einsum(
                "ic,czyx->izyx",
                kernel[row_shift, column_shift],
                piece,
                precision=lax.Precision.HIGHEST,
            )
            summed = term if summed is None else summed + term
    return summed


def transform(real_part, imag_part, pattern, length, inverse):
    index = jnp.arange(length, dtype=jnp.int32)
    angles = (index[:, None] * index[None, :] % length).astype(jnp.float32) * (
        2.0 * math.pi / length
    )
    factor = 1.0 / math.sqrt(length)
    cosine_table = jnp.cos(angles) * factor
    sine_table = jnp.sin(angles) * factor

    def multiply(volume, table):
        return jnp.einsum(pattern, volume, table, precision=lax.Precision.HIGHEST)

    if inverse:
        return (
            multiply(real_part, cosine_table) - multiply(imag_part, sine_table),
            multiply(imag_part, cosine_table) + multiply(real_part, sine_table),
        )
    return (
        multiply(real_part, cosine_table) + multiply(imag_part, sine_table),
        multiply(imag_part, cosine_table) - multiply(real_part, sine_table),
    )


def depth_forward(pieces):
    real_part, imag_part = transform(pieces[0], pieces[1], "czyx,zk->ckyx", pieces.shape[2], False)
    return jnp.stack([real_part, imag_part])


def plane_inverse(pieces):
    real_part, imag_part = transform(pieces[0], pieces[1], "czyx,yk->czkx", pieces.shape[3], True)
    real_part, imag_part = transform(real_part, imag_part, "czyx,xk->czyk", pieces.shape[4], True)
    return jnp.stack([real_part, imag_part])


def general_shards(
    estimate, coil_maps, measured, sampled, plane_kernel, depth_kernel, depth_offset
):
    slices = estimate.shape[1]
    image_bf = estimate.astype(jnp.bfloat16)
    features = plane_conv(image_bf, plane_kernel).astype(jnp.bfloat16)
    padded_feat = with_halo(features, (("cuts", 1),), 1)
    preact = depth_offset[:, None, None, None]
    for tap_index in range(3):
        preact = preact + jnp.einsum(
            "ic,izyx->czyx",
            depth_kernel[tap_index],
            padded_feat[:, tap_index : tap_index + slices],
            preferred_element_type=jnp.float32,
        )
    activation = jnp.tanh(preact).astype(jnp.bfloat16)
    plane_wide = plane_kernel.astype(jnp.float32)
    projected = [
        plane_adjoint(
            jnp.einsum(
                "ic,czyx->izyx",
                depth_kernel[tap_index],
                activation,
                preferred_element_type=jnp.float32,
            ),
            plane_wide,
        )
        for tap_index in range(3)
    ]
    from_below = shifted_2(projected[2], "cuts", 1)
    from_above = shifted_2(projected[0], "cuts", -1)
    regular = projected[1] + jnp.concatenate([from_below, projected[2][:, : slices - 1]], axis=1)
    regular = regular + jnp.concatenate([projected[0][:, 1:], from_above], axis=1)
    maps_real, maps_imag = (coil_maps[0], coil_maps[1])
    image_real, image_imag = (estimate[0][None], estimate[1][None])
    coil_real = maps_real * image_real - maps_imag * image_imag
    coil_imag = maps_real * image_imag + maps_imag * image_real
    coil_real, coil_imag = transform(
        coil_real, coil_imag, "czyx,xk->czyk", coil_real.shape[3], False
    )
    coil_real, coil_imag = transform(
        coil_real, coil_imag, "czyx,yk->czkx", coil_real.shape[2], False
    )
    stacked = jnp.stack([coil_real, coil_imag])
    kspace = depth_forward(lax.all_to_all(stacked, "cuts", split_axis=3, concat_axis=2, tiled=True))
    keep_mask = sampled.astype(jnp.float32)[None, None, :, :, None]
    residual = keep_mask * (kspace - measured)
    depth_real, depth_imag = transform(
        residual[0], residual[1], "czyx,zk->ckyx", residual.shape[2], True
    )
    errors = plane_inverse(
        lax.all_to_all(
            jnp.stack([depth_real, depth_imag]), "cuts", split_axis=2, concat_axis=3, tiled=True
        )
    )
    grad_real = jnp.sum(maps_real * errors[0] + maps_imag * errors[1], axis=0)
    grad_imag = jnp.sum(maps_real * errors[1] - maps_imag * errors[0], axis=0)
    gradient = jnp.stack([grad_real, grad_imag])
    return estimate - step_size * gradient - reg_weight * regular


def dft_tables(length):
    index = np.arange(length)
    angles = 2.0 * np.pi * ((index[:, None] * index[None, :]) % length) / length
    factor = 1.0 / np.sqrt(length)
    return np.cos(angles) * factor, np.sin(angles) * factor


def two_parts(table):
    table = table.astype(np.float32)
    high = table.astype(bf16)
    return high, (table - high.astype(np.float32)).astype(bf16)


def line_order(length, devices):
    lines = length // devices
    order = np.arange(2 * length).reshape(2, devices, lines)
    return order.transpose(1, 0, 2).reshape(-1)


def line_table(length, devices, slab):
    cosine, sine = dft_tables(length)
    full = np.block([[cosine, sine], [-sine, cosine]]) / np.sqrt(slab)
    return two_parts(full[line_order(length, devices)])


def line_table_back(length, devices, slab):
    cosine, sine = dft_tables(length)
    full = np.block([[cosine, -sine], [sine, cosine]]) / np.sqrt(slab)
    return two_parts(full[:, line_order(length, devices)])


def readout_table(length):
    cosine, sine = dft_tables(length)
    return two_parts(np.block([[cosine, sine], [-sine, cosine]]))


def fft_list(real, imag, sign):
    count = len(real)
    if count == 1:
        return real, imag
    even_r, even_i = fft_list(real[0::2], imag[0::2], sign)
    odd_r, odd_i = fft_list(real[1::2], imag[1::2], sign)
    half = count // 2
    low_r, low_i, high_r, high_i = [], [], [], []
    for k in range(half):
        a, b = odd_r[k], odd_i[k]
        if k == 0:
            tr, ti = a, b
        elif 4 * k == count:
            tr, ti = (b, -a) if sign < 0 else (-b, a)
        elif 8 * k == count or 8 * k == 3 * count:
            h = math.sqrt(0.5)
            c = h if 8 * k == count else -h
            s = sign * h
            if c > 0:
                tr, ti = ((a - b) * h, (a + b) * h) if s > 0 else ((a + b) * h, (b - a) * h)
            else:
                tr, ti = ((a + b) * (-h), (a - b) * h) if s > 0 else ((b - a) * h, (a + b) * (-h))
        else:
            c = math.cos(2.0 * math.pi * k / count)
            s = sign * math.sin(2.0 * math.pi * k / count)
            tr, ti = a * c - b * s, a * s + b * c
        low_r.append(even_r[k] + tr)
        low_i.append(even_i[k] + ti)
        high_r.append(even_r[k] - tr)
        high_i.append(even_i[k] - ti)
    return low_r + high_r, low_i + high_i


def dot(a, b):
    return jnp.dot(a, b, preferred_element_type=f32)


def whole_block(shape):
    return pl.BlockSpec(shape, lambda *_: (0,) * len(shape))


def coil_lines(coil_maps, estimate, devices, slab, per_step):
    _, coils, _, rows, columns = coil_maps.shape
    high, low = line_table(rows, devices, slab)

    def kernel(maps_ref, image_ref, high_ref, low_ref, out_ref):
        image_r, image_i = image_ref[0, 0], image_ref[1, 0]
        for c in range(per_step):
            map_r, map_i = maps_ref[0, c, 0], maps_ref[1, c, 0]
            coil = jnp.concatenate(
                [map_r * image_r - map_i * image_i, map_r * image_i + map_i * image_r], axis=0
            ).astype(bf16)
            lines = dot(high_ref[...], coil) + dot(low_ref[...], coil)
            out_ref[:, c] = lines.astype(bf16).reshape(devices, 2 * rows // devices, columns)

    return pl.pallas_call(
        kernel,
        out_shape=jax.ShapeDtypeStruct((devices, coils, 2 * rows // devices, columns), bf16),
        grid=(coils // per_step,),
        in_specs=[
            pl.BlockSpec((2, per_step, 1, rows, columns), lambda i: (0, i, 0, 0, 0)),
            whole_block(estimate.shape),
            whole_block(high.shape),
            whole_block(low.shape),
        ],
        out_specs=pl.BlockSpec(
            (devices, per_step, 2 * rows // devices, columns), lambda i: (0, i, 0, 0)
        ),
        name="coil_lines",
    )(coil_maps, estimate, high, low)


def measured_readout(measured, keep, per_step):
    _, coils, slab, lines, columns = measured.shape
    high, low = readout_table(columns)

    def kernel(data_ref, keep_ref, high_ref, low_ref, out_ref):
        rows = per_step * slab * lines
        data = jnp.concatenate(
            [data_ref[0].reshape(rows, columns), data_ref[1].reshape(rows, columns)], axis=1
        ).astype(bf16)
        result = dot(data, high_ref[...]) + dot(data, low_ref[...])
        for part in range(2):
            piece = result[:, part * columns : (part + 1) * columns]
            piece = piece.reshape(per_step, slab, lines, columns)
            for at in (slice(i, i + 128) for i in range(0, columns, 128)):
                out_ref[:, :, part, :, at] = keep_ref[...] * piece[:, :, :, at]

    return pl.pallas_call(
        kernel,
        out_shape=jax.ShapeDtypeStruct((coils, slab, 2, lines, columns), f32),
        grid=(coils // per_step,),
        in_specs=[
            pl.BlockSpec((2, per_step, slab, lines, columns), lambda i: (0, i, 0, 0, 0)),
            whole_block(keep.shape),
            whole_block(high.shape),
            whole_block(low.shape),
        ],
        out_specs=pl.BlockSpec((per_step, slab, 2, lines, columns), lambda i: (i, 0, 0, 0, 0)),
        name="measured_readout",
    )(measured, keep, high, low)


def depth_residual(lines_in, readout, keep, per_step):
    slab, coils, double, columns = lines_in.shape
    lines = double // 2
    width = 128

    def kernel(in_ref, data_ref, keep_ref, out_ref):
        def one(step, carry):
            c = step // (columns // width)
            coil = pl.program_id(0) * per_step + c
            at = pl.ds(pl.multiple_of((step % (columns // width)) * width, width), width)
            loaded = [in_ref[z, coil, :, at].astype(f32) for z in range(slab)]
            real, imag = fft_list([v[:lines] for v in loaded], [v[lines:] for v in loaded], -1)
            for k in range(slab):
                mask = keep_ref[k]
                real[k] = mask * real[k] - data_ref[c, k, 0, :, at]
                imag[k] = mask * imag[k] - data_ref[c, k, 1, :, at]
            real, imag = fft_list(real, imag, 1)
            for z in range(slab):
                out_ref[z, c, :, at] = jnp.concatenate([real[z], imag[z]], axis=0).astype(bf16)
            return carry

        lax.fori_loop(0, per_step * (columns // width), one, 0)

    return pl.pallas_call(
        kernel,
        out_shape=jax.ShapeDtypeStruct(lines_in.shape, bf16),
        grid=(coils // per_step,),
        in_specs=[
            pl.BlockSpec(memory_space=pltpu.VMEM),
            pl.BlockSpec((per_step, slab, 2, lines, columns), lambda i: (i, 0, 0, 0, 0)),
            whole_block(keep.shape),
        ],
        out_specs=pl.BlockSpec((slab, per_step, double, columns), lambda i: (0, i, 0, 0)),
        name="depth_residual",
    )(pltpu.with_memory_space_constraint(lines_in, pltpu.VMEM), readout, keep)


def image_update(lines_back, coil_maps, estimate, regular, slab, per_step):
    devices, coils, double, columns = lines_back.shape
    rows = coil_maps.shape[3]
    high, low = line_table_back(rows, devices, slab)

    def kernel(lines_ref, maps_ref, image_ref, regular_ref, high_ref, low_ref, out_ref):
        step = pl.program_id(0)

        @pl.when(step == 0)
        def _():
            out_ref[...] = image_ref[...] - reg_weight * regular_ref[...]

        sum_r = sum_i = None
        for c in range(per_step):
            lines = lines_ref[:, step * per_step + c].reshape(devices * double, columns)
            errors = dot(high_ref[...], lines) + dot(low_ref[...], lines)
            error_r, error_i = errors[:rows], errors[rows:]
            map_r, map_i = maps_ref[0, c, 0], maps_ref[1, c, 0]
            term_r = map_r * error_r + map_i * error_i
            term_i = map_r * error_i - map_i * error_r
            sum_r = term_r if sum_r is None else sum_r + term_r
            sum_i = term_i if sum_i is None else sum_i + term_i
        out_ref[0, 0] = out_ref[0, 0] - step_size * sum_r
        out_ref[1, 0] = out_ref[1, 0] - step_size * sum_i

    return pl.pallas_call(
        kernel,
        out_shape=jax.ShapeDtypeStruct(estimate.shape, f32),
        grid=(coils // per_step,),
        in_specs=[
            pl.BlockSpec(memory_space=pltpu.VMEM),
            pl.BlockSpec((2, per_step, 1, rows, columns), lambda i: (0, i, 0, 0, 0)),
            whole_block(estimate.shape),
            whole_block(regular.shape),
            whole_block(high.shape),
            whole_block(low.shape),
        ],
        out_specs=whole_block(estimate.shape),
        name="image_update",
    )(pltpu.with_memory_space_constraint(lines_back, pltpu.VMEM), coil_maps, estimate, regular, high, low)


def regularizer(images, plane_kernel, depth_kernel, depth_offset, columns):
    points = images.shape[1]
    channels = plane_kernel.shape[3]
    block = 2048 if points % 2048 == 0 else columns
    plane_wide = plane_kernel.astype(f32).reshape(9, 2, channels)
    depth_wide = depth_kernel.astype(f32)
    spread = jnp.eye(3, dtype=f32)
    features_of = jnp.einsum("st,ric->scrti", spread, plane_wide).reshape(3 * channels, 9, 6)
    features_of = jnp.pad(features_of, ((0, 0), (0, 0), (0, 2)))
    features_of = features_of.reshape(3 * channels, 72).astype(bf16)
    mix = depth_wide.transpose(2, 0, 1).reshape(channels, 3 * channels).astype(bf16)
    back = jnp.einsum("rij,kjc->rkic", plane_wide, depth_wide, precision=lax.Precision.HIGHEST)
    back = jnp.pad(back.reshape(9, 6, channels), ((0, 0), (0, 2), (0, 0))).reshape(72, channels)
    back_high = back.astype(bf16)
    back_low = (back - back_high.astype(f32)).astype(bf16)
    offset = jnp.broadcast_to(depth_offset[:, None], (channels, 128))

    def kernel(image_ref, features_ref, mix_ref, high_ref, low_ref, offset_ref, out_ref, taps_ref, sums_ref):
        image = image_ref[...].astype(f32)
        column = lax.broadcasted_iota(jnp.int32, (8, points), 1) % columns
        edge = jnp.zeros((8, columns), f32)
        left = jnp.where(column == 0, 0.0, pltpu.roll(image, 1, 1))
        right = jnp.where(column == columns - 1, 0.0, pltpu.roll(image, points - 1, 1))
        for b, moved in enumerate((left, image, right)):
            taps_ref[b, :, :columns] = edge
            taps_ref[b, :, columns : columns + points] = moved
            taps_ref[b, :, columns + points :] = edge
        sums_ref[...] = jnp.zeros(sums_ref.shape, f32)
        bias = offset_ref[:, :1]

        def one(j, carry):
            def at(a):
                return pl.ds(pl.multiple_of(j * block + a * columns, 128), block)

            taps = jnp.concatenate(
                [taps_ref[b, :, at(a)] for a in range(3) for b in range(3)], axis=0
            ).astype(bf16)
            features = dot(features_ref[...], taps).astype(bf16)
            activation = jnp.tanh(dot(mix_ref[...], features) + bias).astype(bf16)
            spread_back = dot(high_ref[...], activation) + dot(low_ref[...], activation)
            for a in range(3):
                for b in range(3):
                    row = 8 * (3 * a + b)
                    sums_ref[b, :, at(a)] = sums_ref[b, :, at(a)] + spread_back[row : row + 8]
            return carry

        lax.fori_loop(0, points // block, one, 0)
        inside = slice(columns, columns + points)
        from_right = pltpu.roll(sums_ref[0, :, inside], points - 1, 1)
        from_left = pltpu.roll(sums_ref[2, :, inside], 1, 1)
        out_ref[...] = (
            sums_ref[1, :, inside]
            + jnp.where(column == columns - 1, 0.0, from_right)
            + jnp.where(column == 0, 0.0, from_left)
        )

    padded = points + 2 * columns
    return pl.pallas_call(
        kernel,
        out_shape=jax.ShapeDtypeStruct((8, points), f32),
        scratch_shapes=[pltpu.VMEM((3, 8, padded), f32), pltpu.VMEM((3, 8, padded), f32)],
        name="regularizer",
    )(images, features_of, mix, back_high, back_low, offset)


def fast_shards(estimate, coil_maps, measured, sampled, plane_kernel, depth_kernel, depth_offset):
    devices = lax.axis_size("cuts")
    _, coils, _, rows, columns = coil_maps.shape
    slab, lines = sampled.shape
    points = rows * columns
    up = [(i, i + 1) for i in range(devices - 1)]
    down = [(i + 1, i) for i in range(devices - 1)]

    coil_side = coil_lines(coil_maps, estimate, devices, slab, 4)
    line_side = lax.all_to_all(coil_side, "cuts", 0, 0, tiled=True)

    image_bf = estimate.astype(bf16)
    below = lax.ppermute(image_bf, "cuts", up)
    above = lax.ppermute(image_bf, "cuts", down)
    images = jnp.concatenate([below, image_bf, above], axis=0).reshape(6, points)
    images = jnp.pad(images, ((0, 2), (0, 0)))

    keep = jnp.broadcast_to(sampled.astype(f32)[:, :, None], (slab, lines, 128))
    readout = measured_readout(measured, keep, 4)
    residual = depth_residual(line_side, readout, keep, 4)
    lines_back = lax.all_to_all(residual, "cuts", 0, 0, tiled=True)

    images, residual = lax.optimization_barrier((images, residual))
    parts = regularizer(images, plane_kernel, depth_kernel, depth_offset, columns)
    parts = parts[:6].reshape(3, 2, 1, rows, columns)
    regular = parts[1] + lax.ppermute(parts[2], "cuts", up) + lax.ppermute(parts[0], "cuts", down)
    return image_update(lines_back, coil_maps, estimate, regular, slab, 4)


def shards(estimate, coil_maps, measured, sampled, plane_kernel, depth_kernel, depth_offset):
    devices = lax.axis_size("cuts")
    slab, lines = sampled.shape
    coils, slices = coil_maps.shape[1:3]
    fits = (
        slices == 1
        and slab == devices
        and slab & (slab - 1) == 0
        and lines % 8 == 0
        and coils % 4 == 0
        and estimate.shape[3] % 128 == 0
    )
    chosen = fast_shards if fits else general_shards
    return chosen(
        estimate, coil_maps, measured, sampled, plane_kernel, depth_kernel, depth_offset
    )


def solution(mesh):
    return jax.shard_map(
        shards,
        mesh=mesh,
        in_specs=(
            P("groups", "cuts", None, None),
            P("groups", None, "cuts", None, None),
            P("groups", None, None, "cuts", None),
            P("groups", "cuts"),
            P(),
            P(),
            P(),
        ),
        out_specs=P("groups", "cuts", None, None),
        check_vma=False,
    )
```
